32 devices in a mesh: groups: 2 (over y), shard: 4 (over z), pair: 4 (over x, core).
Axes of the slice: x: 2, y: 2, z: 4, core: 2. Of those that a mesh axis runs over, the one named last changes fastest.
Arguments:
- gradient: bfloat16 [2, 8, 512, 512], P('groups', None, 'shard'), parts along dimension 0, may hold values from -6.5 to 6.5, as said below
- momentum: bfloat16 [2, 8, 512, 512], P('groups', None, 'shard'), parts along dimension 0, may hold values from -6.5 to 6.5, as said below
Outputs:
- update: bfloat16 [2, 8, 512, 512], P('groups', None, 'shard'), parts along dimension 0
- new_momentum: bfloat16 [2, 8, 512, 512], P('groups', None, 'shard'), parts along dimension 0
The draws below stay inside these ranges and needn't reach their ends.
There are 2 independent parts, one for each index of `groups`. The reference program is written for one: setup_inputs(seed, part) draws one part's arguments, and reference() takes and returns one part's arrays. A program takes and returns all parts, laid end to end along the dimension named above; each array names one. Nothing has to cross between parts.
Inputs may be any that keep to these rules, and one draw needn't show every extreme that they name: `gradient`: entries of order one. `momentum`: entries of order one.
All inputs are finite; a program needn't handle non-finite values.
Results may differ from the reference program's by a relative error of at most 0.0053.
Values may be sent and summed in bfloat16 or wider, within the bound.
No kernel may reach another device: no remote copies, remote signals or barrier semaphores. Data moves between devices by JAX's collectives and lax.ppermute only.
A program may use at most 64 MiB of HBM per device.

```python
import jax
import jax.numpy as jnp
from jax import lax

BLK = 512
BCOL = 8
BROW = 1


def block_entries(key, salt):
    inner = jax.random.fold_in(key, salt)
    base_key = jax.random.fold_in(inner, 0)
    full_shape = (BROW, BCOL, BLK, BLK)
    values = jax.random.truncated_normal(base_key, -6.0, 6.0, full_shape, jnp.float32)
    return values.astype(jnp.bfloat16)


def draw_gradient(key, part):
    return block_entries(key, 101)


def draw_momentum(key, part):
    return block_entries(key, 202)


def setup_inputs(seed: int = 0, part: int = 0) -> dict:
    splits = jax.random.split(jax.random.key(seed), 3)
    own_keys = jax.random.split(jax.random.fold_in(splits[2], part), 3)
    gradient = draw_gradient(jax.random.fold_in(jax.random.fold_in(splits[2], part), 71), part)
    momentum = draw_momentum(jax.random.fold_in(jax.random.fold_in(splits[2], part), 71), part)
    return {"gradient": gradient, "momentum": momentum}


damping = 0.1
decay_rate = 0.9

def multiply(left_matrix, right_matrix):
    return jnp.dot(left_matrix, right_matrix, precision=lax.Precision.HIGHEST, preferred_element_type=jnp.float32)

def gram_root(gram_matrix):
    block_size = gram_matrix.shape[0]
    identity = jnp.eye(block_size, dtype=jnp.float32)
    scaling = 2.0 * jnp.trace(gram_matrix) / block_size
    root_scale = jnp.sqrt(jnp.sqrt(scaling))
    scaled = gram_matrix / scaling
    leading = (5.0 * identity - scaled) / 4.0
    iterate = leading / root_scale
    squared = multiply(leading, leading)
    fourth = multiply(squared, squared)
    shifted = multiply(fourth, scaled)
    second = (5.0 * identity - shifted) / 4.0
    return multiply(iterate, second)

def reference(gradient, momentum):
    new_momentum = (decay_rate * momentum.astype(jnp.float32) + gradient.astype(jnp.float32)).astype(jnp.bfloat16)
    grad_blocks = gradient.reshape(-1, BLK, BLK)
    mom_blocks = new_momentum.reshape(-1, BLK, BLK)
    identity = jnp.eye(BLK, dtype=jnp.float32)

    def one_block(blocks_pair):
        grad_block, mom_block = blocks_pair
        left_gram = jnp.dot(grad_block, grad_block.T, preferred_element_type=jnp.float32) / BLK + damping * identity
        right_gram = jnp.dot(grad_block.T, grad_block, preferred_element_type=jnp.float32) / BLK + damping * identity
        left_root = gram_root(left_gram)
        right_root = gram_root(right_gram)
        partial_prod = multiply(mom_block.astype(jnp.float32), right_root)
        return multiply(left_root, partial_prod).astype(jnp.bfloat16)
    updates = lax.map(one_block, (grad_blocks, mom_blocks)).reshape(gradient.shape)
    return (updates, new_momentum)
```

```python
import functools

import jax
import jax.numpy as jnp
from jax import lax
from jax.experimental import pallas as pl
from jax.experimental.pallas import tpu as pltpu
from jax.sharding import PartitionSpec as P

damping = 0.1
decay_rate = 0.9


VMEM = pl.BlockSpec(memory_space=pltpu.VMEM)
SMEM = pl.BlockSpec(memory_space=pltpu.SMEM)
ANY = pl.BlockSpec(memory_space=pl.ANY)


def from_partner(value, axis, mask):
    pairs = [(source, source ^ mask) for source in range(lax.axis_size(axis))]
    return lax.ppermute(value, axis, pairs)


def place():
    position = lax.axis_index("pair")
    return position // 2, position % 2, lax.axis_index("shard")


def matmul(left, right):
    return jnp.dot(left, right, preferred_element_type=jnp.float32)


def pick_kernel(distances, shards, half_rows, array, *rest):
    outs, sems = rest[:-1], rest[-1]
    half, core, shard = place()
    copies = []
    for number, distance in enumerate(distances):
        block = half * shards + (shard ^ distance)
        if distance:
            source = array.at[block, pl.ds(pl.multiple_of(core * half_rows, half_rows), half_rows)]
        else:
            source = array.at[block]
        copies.append(pltpu.make_async_copy(source, outs[number], sems.at[number]))
    for copy in copies:
        copy.start()
    for copy in copies:
        copy.wait()


def pick(array, distances, shards):
    _, rows, width = array.shape
    shapes = [
        jax.ShapeDtypeStruct((rows // 2 if distance else rows, width), array.dtype)
        for distance in distances
    ]
    return pl.pallas_call(
        functools.partial(pick_kernel, distances, shards, rows // 2),
        out_shape=shapes,
        in_specs=[ANY],
        out_specs=[VMEM] * len(shapes),
        scratch_shapes=[pltpu.SemaphoreType.DMA((len(shapes),))],
        name="pick",
    )(array)


def fill(target, own, mine, other, core, half_rows, value):
    count = len(mine) + 1
    keep = pl.ds(pl.multiple_of(core * half_rows, half_rows), half_rows)
    rest = pl.ds(pl.multiple_of((1 - core) * half_rows, half_rows), half_rows)
    target[0:half_rows, :] = value(own, 0, keep)
    target[count * half_rows : (count + 1) * half_rows, :] = value(own, 0, rest)
    for number in range(1, count):
        start = number * half_rows
        target[start : start + half_rows, :] = value(mine, number, None)
        start = (count + number) * half_rows
        target[start : start + half_rows, :] = value(other, number, None)


def root_parts(gram, scaling, rows):
    size = gram.shape[0]
    line = lax.broadcasted_iota(jnp.int32, (size, size), 0)
    identity = line == lax.broadcasted_iota(jnp.int32, (size, size), 1)
    excess = gram / scaling + jnp.where(identity, damping / scaling - 0.5, 0.0)
    excess_low = excess.astype(jnp.bfloat16)
    squared = matmul(excess_low, excess_low)
    alpha, beta = 1.265625, 0.5625
    shift = squared * 0.0625 - excess * 0.5625
    shift_low = shift.astype(jnp.bfloat16)
    product = excess - 0.25 * squared
    fourth = matmul(shift_low[:rows], shift_low) + (2.0 * alpha) * shift[:rows]
    last = matmul(fourth.astype(jnp.bfloat16), product.astype(jnp.bfloat16))
    return -1.25 * excess[:rows] - (alpha * alpha) * product[:rows] - beta * fourth - last


def root_kernel(count, own, *rest):
    mine, other = (None,) + rest[: count - 1], (None,) + rest[count - 1 : 2 * count - 2]
    left_ref, right_ref, rho_ref, block = rest[2 * count - 2 :]
    half, core, shard = place()
    half_rows = own.shape[0] // 2
    read = lambda refs, number, keep: refs[keep, :] if keep is not None else refs[number][...]
    fill(block, own, mine[1:], other[1:], core, half_rows, lambda refs, number, keep: (
        refs[keep, :] if keep is not None else refs[number - 1][...]))
    finish_roots(block, left_ref, right_ref, rho_ref)


def finish_roots(block, left_ref, right_ref, rho_ref):
    size = block.shape[0]
    values = block[...]
    flipped = values.T
    wide = values.astype(jnp.float32)
    total = jnp.sum(wide * wide)
    scaling = 2.0 * (total / size + damping * size) / size
    scaling = jnp.full((1, 1), scaling, jnp.float32)
    root_scale = jnp.sqrt(jnp.sqrt(scaling))
    alpha, beta = 1.265625, 0.5625
    rho_ref[...] = jnp.broadcast_to((5.625 - alpha * alpha * beta) / (4.0 * root_scale), rho_ref.shape)
    weight = 0.25 / root_scale
    right = root_parts(matmul(flipped, values) / size, scaling, size)
    right_ref[...] = (right * weight).astype(jnp.bfloat16)
    rows = left_ref.shape[0]
    left = root_parts(matmul(values, flipped) / size, scaling, rows)
    left_ref[...] = (left * weight).astype(jnp.bfloat16)


def update_kernel(count, left_ref, right_ref, rho_ref, *rest):
    grads, moms = rest[: 2 * count - 1], rest[2 * count - 1 : 4 * count - 2]
    outs, block = rest[4 * count - 2 : -1], rest[-1]
    half, core, shard = place()
    half_rows = grads[0].shape[0] // 2

    def value(refs, number, keep):
        grad, mom = refs
        if keep is not None:
            grad, mom = grad[keep, :], mom[keep, :]
        else:
            grad, mom = grad[number - 1][...], mom[number - 1][...]
        fresh = decay_rate * mom.astype(jnp.float32) + grad.astype(jnp.float32)
        return fresh.astype(jnp.bfloat16)

    fill(
        block,
        (grads[0], moms[0]),
        Both(grads[1:count], moms[1:count]),
        Both(grads[count:], moms[count:]),
        core,
        half_rows,
        value,
    )
    rho = rho_ref[0:1, 0:1]
    values = block[...]
    partial = rho * values.astype(jnp.float32) + matmul(values, right_ref[...])
    rows = left_ref.shape[0]
    result = rho * partial[:rows] + matmul(left_ref[...], partial.astype(jnp.bfloat16))
    result = result.astype(jnp.bfloat16)
    for number, out in enumerate(outs):
        out[...] = result[number * half_rows : (number + 1) * half_rows]


class Both(tuple):
    def __new__(cls, *parts):
        return super().__new__(cls, parts)

    def __len__(self):
        return len(self[0])


def join_kernel(count, *rest):
    pieces, out, sems = rest[: 4 * count], rest[-2], rest[-1]
    half, core, shard = place()
    half_rows = pieces[0].shape[0]
    copies = []
    for kind in range(4):
        side = half if kind % 2 == 0 else 1 - half
        part = core if kind < 2 else 1 - core
        for distance in range(count):
            number = kind * count + distance
            rows = pl.ds(pl.multiple_of(part * half_rows, half_rows), half_rows)
            target = out.at[side * count + (shard ^ distance), rows]
            copies.append(pltpu.make_async_copy(pieces[number], target, sems.at[number]))
    for copy in copies:
        copy.start()
    for copy in copies:
        copy.wait()


def direct(gradient, momentum, shards):
    block_rows, block_cols, rows, size = gradient.shape
    half_rows = rows // 2
    grad = gradient.reshape(-1, rows, size)
    mom = momentum.reshape(-1, rows, size)
    far = list(range(1, shards))
    grad_out = pick(grad, far, shards)
    grad_mine = [from_partner(v, "shard", d) for v, d in zip(grad_out, far)]
    grad_other = [from_partner(v, "pair", 1) for v in grad_mine]
    (grad_own,) = pick(grad, [0], shards)
    mom_out = pick(mom, [0] + far, shards)
    mom_own, mom_out = mom_out[0], mom_out[1:]
    mom_mine = [from_partner(v, "shard", d) for v, d in zip(mom_out, far)]
    mom_other = [from_partner(v, "pair", 1) for v in mom_mine]
    kept = shards * half_rows
    left, right, rho = pl.pallas_call(
        functools.partial(root_kernel, shards),
        out_shape=[
            jax.ShapeDtypeStruct((kept, size), jnp.bfloat16),
            jax.ShapeDtypeStruct((size, size), jnp.bfloat16),
            jax.ShapeDtypeStruct((8, 128), jnp.float32),
        ],
        in_specs=[VMEM] * (2 * shards - 1),
        out_specs=[VMEM] * 3,
        scratch_shapes=[pltpu.VMEM((size, size), jnp.bfloat16)],
        name="roots",
    )(grad_own, *grad_mine, *grad_other)
    pieces = pl.pallas_call(
        functools.partial(update_kernel, shards),
        out_shape=[jax.ShapeDtypeStruct((half_rows, size), jnp.bfloat16)] * shards,
        in_specs=[VMEM] * (4 * shards + 1),
        out_specs=[VMEM] * shards,
        scratch_shapes=[pltpu.VMEM((size, size), jnp.bfloat16)],
        name="update",
    )(left, right, rho, grad_own, *grad_mine, *grad_other, mom_own, *mom_mine, *mom_other)
    mine = [pieces[0]] + [from_partner(v, "shard", d) for v, d in zip(pieces[1:], far)]
    across = [from_partner(v, "pair", 2) for v in mine]
    swapped = [from_partner(v, "pair", 1) for v in mine + across]
    update = pl.pallas_call(
        functools.partial(join_kernel, shards),
        out_shape=jax.ShapeDtypeStruct(grad.shape, jnp.bfloat16),
        in_specs=[VMEM] * (4 * shards),
        out_specs=ANY,
        scratch_shapes=[pltpu.SemaphoreType.DMA((4 * shards,))],
        name="join",
    )(*mine, *across, *swapped)
    return update.reshape(gradient.shape)


def general(gradient, new_momentum, shards):
    block_rows, block_cols, rows, size = gradient.shape
    half_cols, half_width = block_cols // 2, size // 2
    half, core, shard = place()

    def collect(array):
        array = lax.dynamic_slice_in_dim(array, half * half_cols, half_cols, 1)
        array = array.reshape(shards, rows, size)
        array = lax.all_to_all(array, "shard", split_axis=0, concat_axis=1, tiled=True)
        return array[0]

    grad_block, mom_block = collect(gradient), collect(new_momentum)
    left, right, rho = pl.pallas_call(
        finish_roots,
        out_shape=[
            jax.ShapeDtypeStruct((size, size), jnp.bfloat16),
            jax.ShapeDtypeStruct((size, size), jnp.bfloat16),
            jax.ShapeDtypeStruct((8, 128), jnp.float32),
        ],
        in_specs=[VMEM],
        out_specs=[VMEM] * 3,
        name="roots",
    )(grad_block)
    rho = rho[0, 0]
    start = core * half_width
    right = lax.dynamic_slice_in_dim(right, start, half_width, 1)
    same = lax.dynamic_slice_in_dim(mom_block, start, half_width, 1)
    partial = rho * same.astype(jnp.float32) + matmul(mom_block, right)
    piece = rho * partial + matmul(left, partial.astype(jnp.bfloat16))
    outgoing = piece.astype(jnp.bfloat16).reshape(shards, rows, half_width)
    returned = lax.all_to_all(outgoing, "shard", split_axis=0, concat_axis=0, tiled=True)
    own_rows = returned.reshape(block_rows, half_cols, rows, half_width)
    gathered = lax.all_gather(own_rows[None], "pair", axis=0, tiled=True)
    return (
        gathered.reshape(2, 2, block_rows, half_cols, rows, half_width)
        .transpose(2, 0, 3, 4, 1, 5)
        .reshape(gradient.shape)
    )


def local(gradient, momentum):
    new_momentum = (
        decay_rate * momentum.astype(jnp.float32) + gradient.astype(jnp.float32)
    ).astype(jnp.bfloat16)
    shards = lax.axis_size("shard")
    rows = gradient.shape[2]
    few = shards <= 8 and shards & (shards - 1) == 0
    if few and rows % 32 == 0:
        return direct(gradient, momentum, shards), new_momentum
    return general(gradient, new_momentum, shards), new_momentum


def solution(mesh):
    specs = (P("groups", None, "shard", None), P("groups", None, "shard", None))
    return jax.shard_map(local, mesh=mesh, in_specs=specs, out_specs=specs, check_vma=False)
```

```python
import functools

import jax
import jax.numpy as jnp
from jax import lax
from jax.experimental import pallas as pl
from jax.experimental.pallas import tpu as pltpu
from jax.sharding import PartitionSpec as P

damping = 0.1
decay_rate = 0.9


VMEM = pl.BlockSpec(memory_space=pltpu.VMEM)
SMEM = pl.BlockSpec(memory_space=pltpu.SMEM)
ANY = pl.BlockSpec(memory_space=pl.ANY)
SMALL = pltpu.CompilerParams(vmem_limit_bytes=16 * 1024 * 1024)


def from_partner(value, axis, mask):
    pairs = [(source, source ^ mask) for source in range(lax.axis_size(axis))]
    return lax.ppermute(value, axis, pairs)


def place():
    position = lax.axis_index("pair")
    return position // 2, position % 2, lax.axis_index("shard")


def matmul(left, right):
    return jnp.dot(left, right, preferred_element_type=jnp.float32)


def pick_kernel(distances, shards, half_rows, array, *rest):
    outs, sems = rest[:-1], rest[-1]
    half, core, shard = place()
    copies = []
    for number, distance in enumerate(distances):
        block = half * shards + (shard ^ distance)
        if distance:
            source = array.at[block, pl.ds(pl.multiple_of(core * half_rows, half_rows), half_rows)]
        else:
            source = array.at[block]
        copies.append(pltpu.make_async_copy(source, outs[number], sems.at[number]))
    for copy in copies:
        copy.start()
    for copy in copies:
        copy.wait()


def pick(array, distances, shards):
    _, rows, width = array.shape
    shapes = [
        jax.ShapeDtypeStruct((rows // 2 if distance else rows, width), array.dtype)
        for distance in distances
    ]
    return pl.pallas_call(
        functools.partial(pick_kernel, distances, shards, rows // 2),
        out_shape=shapes,
        in_specs=[ANY],
        out_specs=[VMEM] * len(shapes),
        scratch_shapes=[pltpu.SemaphoreType.DMA((len(shapes),))],
        compiler_params=SMALL,
        name="pick",
    )(array)


def fill(target, own, mine, other, core, half_rows, value):
    count = len(mine) + 1
    keep = pl.ds(pl.multiple_of(core * half_rows, half_rows), half_rows)
    rest = pl.ds(pl.multiple_of((1 - core) * half_rows, half_rows), half_rows)
    target[0:half_rows, :] = value(own, 0, keep)
    target[count * half_rows : (count + 1) * half_rows, :] = value(own, 0, rest)
    for number in range(1, count):
        start = number * half_rows
        target[start : start + half_rows, :] = value(mine, number, None)
        start = (count + number) * half_rows
        target[start : start + half_rows, :] = value(other, number, None)


def root_parts(gram, scaling, rows):
    size = gram.shape[0]
    line = lax.broadcasted_iota(jnp.int32, (size, size), 0)
    identity = line == lax.broadcasted_iota(jnp.int32, (size, size), 1)
    excess = gram / scaling + jnp.where(identity, damping / scaling - 0.5, 0.0)
    excess_low = excess.astype(jnp.bfloat16)
    squared = matmul(excess_low, excess_low)
    alpha, beta = 1.265625, 0.5625
    shift = squared * 0.0625 - excess * 0.5625
    shift_low = shift.astype(jnp.bfloat16)
    product = excess - 0.25 * squared
    fourth = matmul(shift_low[:rows], shift_low) + (2.0 * alpha) * shift[:rows]
    last = matmul(fourth.astype(jnp.bfloat16), product.astype(jnp.bfloat16))
    return -1.25 * excess[:rows] - (alpha * alpha) * product[:rows] - beta * fourth - last


def root_kernel(count, own, *rest):
    mine, other = rest[: count - 1], rest[count - 1 : 2 * count - 2]
    left_ref, right_ref, rho_ref, block = rest[2 * count - 2 :]
    half, core, shard = place()
    half_rows = own.shape[0] // 2

    def value(refs, number, keep):
        return refs[keep, :] if keep is not None else refs[number - 1][...]

    fill(block, own, mine, other, core, half_rows, value)
    finish_roots(block, left_ref, right_ref, rho_ref)


def finish_roots(block, left_ref, right_ref, rho_ref):
    size = block.shape[0]
    values = block[...]
    flipped = values.T
    wide = values.astype(jnp.float32)
    total = jnp.sum(wide * wide)
    scaling = 2.0 * (total / size + damping * size) / size
    scaling = jnp.full((1, 1), scaling, jnp.float32)
    root_scale = jnp.sqrt(jnp.sqrt(scaling))
    alpha, beta = 1.265625, 0.5625
    rho_ref[...] = jnp.broadcast_to((5.625 - alpha * alpha * beta) / (4.0 * root_scale), rho_ref.shape)
    weight = 0.25 / root_scale
    right = root_parts(matmul(flipped, values) / size, scaling, size)
    right_ref[...] = (right * weight).astype(jnp.bfloat16)
    rows = left_ref.shape[0]
    left = root_parts(matmul(values, flipped) / size, scaling, rows)
    left_ref[...] = (left * weight).astype(jnp.bfloat16)


def update_kernel(count, left_ref, right_ref, rho_ref, *rest):
    grads, moms = rest[: 2 * count - 1], rest[2 * count - 1 : 4 * count - 2]
    outs, block = rest[4 * count - 2 : -1], rest[-1]
    half, core, shard = place()
    half_rows = grads[0].shape[0] // 2

    def value(refs, number, keep):
        grad, mom = refs
        if keep is not None:
            grad, mom = grad[keep, :], mom[keep, :]
        else:
            grad, mom = grad[number - 1][...], mom[number - 1][...]
        fresh = decay_rate * mom.astype(jnp.float32) + grad.astype(jnp.float32)
        return fresh.astype(jnp.bfloat16)

    fill(
        block,
        (grads[0], moms[0]),
        Both(grads[1:count], moms[1:count]),
        Both(grads[count:], moms[count:]),
        core,
        half_rows,
        value,
    )
    rho = rho_ref[0:1, 0:1]
    values = block[...]
    partial = rho * values.astype(jnp.float32) + matmul(values, right_ref[...])
    rows = left_ref.shape[0]
    result = rho * partial[:rows] + matmul(left_ref[...], partial.astype(jnp.bfloat16))
    result = result.astype(jnp.bfloat16)
    for number, out in enumerate(outs):
        out[...] = result[number * half_rows : (number + 1) * half_rows]


class Both(tuple):
    def __new__(cls, *parts):
        return super().__new__(cls, parts)

    def __len__(self):
        return len(self[0])


def join_kernel(count, *rest):
    pieces, out, sems = rest[: 4 * count], rest[-2], rest[-1]
    half, core, shard = place()
    half_rows = pieces[0].shape[0]
    copies = []
    for kind in range(4):
        side = half if kind % 2 == 0 else 1 - half
        part = core if kind < 2 else 1 - core
        for distance in range(count):
            number = kind * count + distance
            rows = pl.ds(pl.multiple_of(part * half_rows, half_rows), half_rows)
            target = out.at[side * count + (shard ^ distance), rows]
            copies.append(pltpu.make_async_copy(pieces[number], target, sems.at[number]))
    for copy in copies:
        copy.start()
    for copy in copies:
        copy.wait()


def direct(gradient, momentum, shards):
    block_rows, block_cols, rows, size = gradient.shape
    half_rows = rows // 2
    grad = gradient.reshape(-1, rows, size)
    mom = momentum.reshape(-1, rows, size)
    far = list(range(1, shards))
    grad_out = pick(grad, far, shards)
    grad_mine = [from_partner(v, "shard", d) for v, d in zip(grad_out, far)]
    grad_other = [from_partner(v, "pair", 1) for v in grad_mine]
    (grad_own,) = pick(grad, [0], shards)
    mom_out = pick(mom, [0] + far, shards)
    mom_own, mom_out = mom_out[0], mom_out[1:]
    mom_mine = [from_partner(v, "shard", d) for v, d in zip(mom_out, far)]
    mom_other = [from_partner(v, "pair", 1) for v in mom_mine]
    kept = shards * half_rows
    left, right, rho = pl.pallas_call(
        functools.partial(root_kernel, shards),
        out_shape=[
            jax.ShapeDtypeStruct((kept, size), jnp.bfloat16),
            jax.ShapeDtypeStruct((size, size), jnp.bfloat16),
            jax.ShapeDtypeStruct((8, 128), jnp.float32),
        ],
        in_specs=[VMEM] * (2 * shards - 1),
        out_specs=[VMEM] * 3,
        scratch_shapes=[pltpu.VMEM((size, size), jnp.bfloat16)],
        compiler_params=SMALL,
        name="roots",
    )(grad_own, *grad_mine, *grad_other)
    pieces = pl.pallas_call(
        functools.partial(update_kernel, shards),
        out_shape=[jax.ShapeDtypeStruct((half_rows, size), jnp.bfloat16)] * shards,
        in_specs=[VMEM] * (4 * shards + 1),
        out_specs=[VMEM] * shards,
        scratch_shapes=[pltpu.VMEM((size, size), jnp.bfloat16)],
        compiler_params=SMALL,
        name="update",
    )(left, right, rho, grad_own, *grad_mine, *grad_other, mom_own, *mom_mine, *mom_other)
    mine = [pieces[0]] + [from_partner(v, "shard", d) for v, d in zip(pieces[1:], far)]
    across = [from_partner(v, "pair", 2) for v in mine]
    swapped = [from_partner(v, "pair", 1) for v in mine + across]
    update = pl.pallas_call(
        functools.partial(join_kernel, shards),
        out_shape=jax.ShapeDtypeStruct(grad.shape, jnp.bfloat16),
        in_specs=[VMEM] * (4 * shards),
        out_specs=ANY,
        scratch_shapes=[pltpu.SemaphoreType.DMA((4 * shards,))],
        compiler_params=SMALL,
        name="join",
    )(*mine, *across, *swapped)
    return update.reshape(gradient.shape)


def general(gradient, new_momentum, shards):
    block_rows, block_cols, rows, size = gradient.shape
    half_cols, half_width = block_cols // 2, size // 2
    half, core, shard = place()

    def collect(array):
        array = lax.dynamic_slice_in_dim(array, half * half_cols, half_cols, 1)
        array = array.reshape(shards, rows, size)
        array = lax.all_to_all(array, "shard", split_axis=0, concat_axis=1, tiled=True)
        return array[0]

    grad_block, mom_block = collect(gradient), collect(new_momentum)
    left, right, rho = pl.pallas_call(
        finish_roots,
        out_shape=[
            jax.ShapeDtypeStruct((size, size), jnp.bfloat16),
            jax.ShapeDtypeStruct((size, size), jnp.bfloat16),
            jax.ShapeDtypeStruct((8, 128), jnp.float32),
        ],
        in_specs=[VMEM],
        out_specs=[VMEM] * 3,
        compiler_params=SMALL,
        name="roots",
    )(grad_block)
    rho = rho[0, 0]
    start = core * half_width
    right = lax.dynamic_slice_in_dim(right, start, half_width, 1)
    same = lax.dynamic_slice_in_dim(mom_block, start, half_width, 1)
    partial = rho * same.astype(jnp.float32) + matmul(mom_block, right)
    piece = rho * partial + matmul(left, partial.astype(jnp.bfloat16))
    outgoing = piece.astype(jnp.bfloat16).reshape(shards, rows, half_width)
    returned = lax.all_to_all(outgoing, "shard", split_axis=0, concat_axis=0, tiled=True)
    own_rows = returned.reshape(block_rows, half_cols, rows, half_width)
    gathered = lax.all_gather(own_rows[None], "pair", axis=0, tiled=True)
    return (
        gathered.reshape(2, 2, block_rows, half_cols, rows, half_width)
        .transpose(2, 0, 3, 4, 1, 5)
        .reshape(gradient.shape)
    )


def local(gradient, momentum):
    new_momentum = (
        decay_rate * momentum.astype(jnp.float32) + gradient.astype(jnp.float32)
    ).astype(jnp.bfloat16)
    shards = lax.axis_size("shard")
    rows = gradient.shape[2]
    few = shards <= 8 and shards & (shards - 1) == 0
    if few and rows % 32 == 0:
        return direct(gradient, momentum, shards), new_momentum
    return general(gradient, new_momentum, shards), new_momentum


def solution(mesh):
    specs = (P("groups", None, "shard", None), P("groups", None, "shard", None))
    return jax.shard_map(local, mesh=mesh, in_specs=specs, out_specs=specs, check_vma=False)
```
